32 devices in a mesh: wave: 4 (over z), tile: 8 (over y, x, core).
Axes of the slice: x: 2, y: 2, z: 4, core: 2. Of those that a mesh axis runs over, the one named last changes fastest.
Arguments:
- spectral: bfloat16 [640, 2, 64, 1281], P('wave', None, 'tile'), may hold values from -0.083496094 to 0.083496094
- legendre: bfloat16 [640, 8, 1281], P('wave'), may hold values from -0.25 to 0.25
- pair_ids: int32 [640], replicated, may hold values from 0 to 639, each once
Outputs:
- spectral_out: bfloat16 [640, 2, 64, 1281], P('wave', None, 'tile')
The draws below stay inside these ranges and needn't reach their ends.
Inputs may be any that keep to these rules, and one draw needn't show every extreme that they name: A permutation: each pair 0 to 639 appears once; slot s of spectral, legendre and spectral_out holds wavenumbers pair_ids[s] and 1279 - pair_ids[s].
All inputs are finite; a program needn't handle non-finite values.
Results may differ from the reference program's by a relative error of at most 0.0072.
Values may be sent and summed in bfloat16 or wider, within the bound.
A program may use at most 64 MiB of HBM per device.

```python
import math
import jax
import jax.numpy as jnp
from jax import lax

MW = 1280
HALF_LATS = 1280
COLS = 64
PAIRS = 640
NROW = 1281
NLAT = 8
NPTS = 5156


def block_scale(own_key, dims, pieces, smallest, largest):
    level, own = 1.0, jax.random.fold_in(own_key, 6)
    for dim, blocks in pieces:
        heights = jnp.exp(jax.random.uniform(jax.random.fold_in(own, dim), (blocks,), jnp.float32, smallest / len(pieces), largest / len(pieces)))
        level = level * jnp.repeat(heights, dims[dim] // blocks).reshape([-1 if axis == dim else 1 for axis in range(len(dims))])
    return level


def gaussian(rng, extent, scale, most, shards=(), held_as=jnp.bfloat16):
    values = scale * jax.random.normal(rng, extent, jnp.float32)
    if shards:
        values = values * block_scale(rng, extent, shards, -0.22, 0.18)
    return jnp.clip(values, -most, most).astype(held_as)


def setup_inputs(seed: int = 0) -> dict:
    seeds = jax.random.split(jax.random.key(seed), 4)
    return {
        "spectral": gaussian(seeds[0], (PAIRS, 2, COLS, NROW), (0.5 / MW ** 0.5), 0.083496094, ((0, 4), (2, 8))),
        "legendre": gaussian(seeds[1], (PAIRS, NLAT, NROW), (MW // 2) ** -0.5, 0.25, ((0, 4),)),
        "pair_ids": jax.random.permutation(seeds[2], PAIRS).astype(jnp.int32),
    }


def build_table(wavenumbers, local_index, length, inside, synthesis):
    phase_step = wavenumbers[:, None] * local_index[None, :] % length[None, :]
    angles = 2.0 * math.pi * phase_step.astype(jnp.float32) / length[None, :].astype(jnp.float32)
    keep_mask = (2 * wavenumbers[:, None] < length[None, :]) & inside[None, :]
    if synthesis:
        factor = jnp.where(wavenumbers == 0, 1.0, 2.0).astype(jnp.float32)[:, None]
    else:
        factor = jnp.ones((wavenumbers.shape[0], 1), jnp.float32)
    cosine = jnp.where(keep_mask, factor * jnp.cos(angles), 0.0)
    sine_part = jnp.where(keep_mask, -factor * jnp.sin(angles), 0.0)
    return jnp.concatenate([cosine, sine_part], axis=0).astype(jnp.bfloat16)

def cycle_lengths(pair_number, pair_total):
    polar_cycle = pair_number * (HALF_LATS // 2) // pair_total
    cycle_index = jnp.stack([polar_cycle, HALF_LATS - 1 - polar_cycle]).astype(jnp.int32)
    return (cycle_index, 20 + 4 * cycle_index)

def point_layout(points, cycle_len):
    second = points >= cycle_len[0]
    local_index = points - jnp.where(second, cycle_len[0], 0)
    length = jnp.where(second, cycle_len[1], cycle_len[0])
    inside = points < cycle_len[0] + cycle_len[1]
    return (second, local_index, length, inside)

def cycle_scale(cycle_index, cycle_len, lat_count):
    angles = math.pi * (cycle_index.astype(jnp.float32) + 0.5) / (2.0 * HALF_LATS)
    return 40.0 * jnp.sin(angles) / jnp.sqrt(lat_count * cycle_len.astype(jnp.float32))

def grid_products(grid_values):
    layer_count = grid_values.shape[0] // 4
    nodal_samples = grid_values.astype(jnp.float32).reshape(4, layer_count, grid_values.shape[1])
    zonal_velocity = nodal_samples[0]
    meridional_velocity = nodal_samples[1]
    thermal_state = nodal_samples[2]
    moisture_ratio = nodal_samples[3]
    gravity_surface_altitude = lax.cumsum(thermal_state, axis=0, reverse=True) / math.sqrt(layer_count)
    motion_squared_half = 0.5 * (zonal_velocity * zonal_velocity + meridional_velocity * meridional_velocity) + gravity_surface_altitude
    joined_variables = jnp.stack([motion_squared_half, zonal_velocity * thermal_state, meridional_velocity * thermal_state, zonal_velocity * moisture_ratio])
    return joined_variables.reshape(grid_values.shape).astype(jnp.bfloat16)

def reference(spectral, legendre, pair_ids):
    columns = spectral.shape[2]
    row_total = spectral.shape[3]
    lat_count = legendre.shape[1]
    row_index = jnp.arange(row_total, dtype=jnp.int32)
    upper_half = row_index[None, :] >= (MW - pair_ids)[:, None]

    def forward_slot(slot_args):
        table_slot, spec_slot, upper_slot = slot_args
        halves = jnp.stack([jnp.where(upper_slot, 0, spec_slot), jnp.where(upper_slot, spec_slot, 0)])
        result = jnp.einsum('lr,hxcr->lhxc', table_slot.astype(jnp.float32), halves.astype(jnp.float32), precision=lax.Precision.HIGHEST)
        return result.astype(jnp.bfloat16)
    fourier_in = lax.map(forward_slot, (legendre, spectral, upper_half))
    wavenumbers = jnp.concatenate([pair_ids, MW - 1 - pair_ids]).astype(jnp.int32)
    points = jnp.arange(NPTS, dtype=jnp.int32)

    def pair_pass(pair_number):
        cycle_index, cycle_len = cycle_lengths(pair_number, lat_count // 2)
        second, local_index, length, inside = point_layout(points, cycle_len)
        scales = cycle_scale(cycle_index, cycle_len, lat_count)
        lines = lax.dynamic_slice_in_dim(fourier_in, (2 * pair_number).astype(jnp.int32), 2, 1)
        matrix = jnp.transpose(lines, (1, 4, 3, 2, 0)).reshape(2 * columns, 4 * PAIRS)
        synth_table = build_table(wavenumbers, local_index, length, inside, True)
        result = jnp.dot(matrix, synth_table, preferred_element_type=jnp.float32).reshape(2, columns, NPTS)
        grid_values = jnp.where(second[None, :], result[1], result[0]).astype(jnp.bfloat16)
        product = grid_products(grid_values)
        anal_table = build_table(wavenumbers, local_index, length, inside, False)
        split_rows = jnp.concatenate([jnp.where(second[None, :], 0, product), jnp.where(second[None, :], product, 0)], axis=0)
        summed = lax.dot_general(split_rows, anal_table, (((1,), (1,)), ((), ())), preferred_element_type=jnp.float32)
        summed = summed.reshape(2, columns, 4 * PAIRS) * scales[:, None, None]
        return summed.astype(jnp.bfloat16)
    backs = lax.map(pair_pass, jnp.arange(lat_count // 2, dtype=jnp.int32))
    backs = backs.reshape(lat_count // 2, 2, columns, 2, 2, PAIRS)
    back = jnp.transpose(backs, (5, 0, 1, 4, 3, 2)).reshape(PAIRS, lat_count, 2, 2, columns)

    def direct_slot(slot_args):
        table_slot, back_slot, upper_slot = slot_args
        result = jnp.einsum('lr,lhxc->hxcr', table_slot.astype(jnp.float32), back_slot.astype(jnp.float32), precision=lax.Precision.HIGHEST)
        return jnp.where(upper_slot, result[1], result[0]).astype(jnp.bfloat16)
    return lax.map(direct_slot, (legendre, back, upper_half))
```

```python
import functools
import math

import jax
import jax.numpy as jnp
from jax import lax
from jax.sharding import PartitionSpec as P

MW = 1280
HALF_LATS = 1280
PAIRS = 640
NPTS = 5156
LANES = 128
RADIX = 32

F32 = jnp.float32
BF16 = jnp.bfloat16


def cycle_lengths(pair_number, pair_total):
    polar_cycle = pair_number * (HALF_LATS // 2) // pair_total
    cycle_index = jnp.stack([polar_cycle, HALF_LATS - 1 - polar_cycle])
    return (cycle_index, 20 + 4 * cycle_index)


def cycle_scale(cycle_index, cycle_len, lat_count):
    angles = math.pi * (cycle_index.astype(F32) + 0.5) / (2.0 * HALF_LATS)
    return 40.0 * jnp.sin(angles) / jnp.sqrt(lat_count * cycle_len.astype(F32))


def trig(wavenumbers, local_index, length):
    phase = (wavenumbers[:, None] * local_index[None, :]) % length[None, :]
    angles = 2.0 * math.pi * phase.astype(F32) / length[None, :].astype(F32)
    return jnp.cos(angles), jnp.sin(angles)


def tables(local_index, length):
    outer = MW // 2 // RADIX
    a_cos, a_sin = trig(2 * RADIX * lax.iota(jnp.int32, outer), local_index, length)
    b_cos, b_sin = trig(lax.iota(jnp.int32, 2 * RADIX), local_index, length)
    pts = local_index.shape[0]
    b_cos = b_cos.reshape(RADIX, 2, pts).transpose(1, 0, 2)[:, None]
    b_sin = b_sin.reshape(RADIX, 2, pts).transpose(1, 0, 2)[:, None]
    a_cos, a_sin = a_cos[None, :, None], a_sin[None, :, None]
    cos = (a_cos * b_cos - a_sin * b_sin).astype(BF16).reshape(2, MW // 2, pts)
    sin = (a_sin * b_cos + a_cos * b_sin).astype(BF16).reshape(2, MW // 2, pts)
    return cos, sin


def grid_products(grid_values):
    layer_count = grid_values.shape[0] // 4
    u, w, t, q = grid_values.astype(F32).reshape(4, layer_count, grid_values.shape[1])
    level = lax.iota(jnp.int32, layer_count)
    acc, rows = t[layer_count - 1], []
    rows.append(acc)
    for v in range(layer_count - 2, -1, -1):
        acc = acc + t[v]
        rows.append(acc)
    geo = jnp.stack(rows[::-1]) / math.sqrt(layer_count)
    energy = 0.5 * (u * u + w * w) + geo
    return jnp.stack([energy, u * t, w * t, u * q]).reshape(grid_values.shape).astype(BF16)


def local(spectral, legendre, pair_ids):
    slots, _, cols, row_total = spectral.shape
    lat_count = legendre.shape[1]
    tiles = lax.axis_size("tile")
    zero = jnp.zeros((), BF16)
    wave_here = lax.axis_index("wave")
    slot_ids = lax.dynamic_slice_in_dim(pair_ids, wave_here * slots, slots)
    row_index = lax.broadcasted_iota(jnp.int32, (slots, row_total), 1)
    upper = (row_index >= (MW - slot_ids)[:, None])[:, None, :]
    masked = jnp.concatenate(
        [jnp.where(upper, zero, legendre), jnp.where(upper, legendre, zero)], axis=1
    )
    spec = spectral.reshape(slots, 2 * cols, row_total)

    cycle_index, cycle_len = cycle_lengths(wave_here, lat_count // 2)
    scales = cycle_scale(cycle_index, cycle_len, lat_count)
    quarter = NPTS // 4
    step = tiles * LANES // math.gcd(4, tiles) if tiles * LANES // math.gcd(4, tiles) <= 512 else 512
    kpad = -(-quarter // step) * step
    k = lax.iota(jnp.int32, kpad)
    q0 = cycle_len[0] // 4
    second = k >= q0
    inside = k < quarter
    local_index = jnp.where(inside, k - jnp.where(second, q0, 0), 0)
    length = jnp.where(second, cycle_len[1], cycle_len[0])
    cos, sin = tables(local_index, length)

    half = MW // 2
    m_order = jnp.arange(MW, dtype=jnp.int32).reshape(half, 2).T
    quarter_m = half // 2
    m0, m1 = m_order[:, :quarter_m], m_order[:, quarter_m:]
    q_of = jnp.stack([m0, MW - 1 - m1]).reshape(2, half)
    hot = (pair_ids[None, :, None] == q_of[:, None, :]).astype(BF16)

    coefficients = lax.dot_general(
        masked, spec, (((2,), (2,)), ((0,), (0,))), preferred_element_type=F32
    ).astype(BF16).reshape(slots, 2, lat_count, 2 * cols)
    coefficients = coefficients.transpose(2, 1, 3, 0)
    fourier = lax.all_to_all(coefficients, "wave", split_axis=0, concat_axis=3, tiled=True)
    ordered = lax.dot_general(
        fourier, hot, (((3,), (1,)), ((1,), (0,))), preferred_element_type=F32
    )
    ordered = ordered.reshape(2, 2, 2, cols, 2, quarter_m).transpose(4, 2, 1, 3, 0, 5)
    ordered = ordered.reshape(2, 2, 2, cols, half)
    factor = jnp.where(m_order == 0, 1.0, 2.0).astype(F32)
    keep = 2 * m_order[:, None, :] < cycle_len[None, :, None]
    ordered = ordered * jnp.where(keep, factor[:, None, :], 0.0)[:, None, :, None, :]
    sign = jnp.where(m_order // 2 % 2 == 0, 1.0, -1.0).astype(F32)
    re, im = ordered[:, 0].reshape(2, 2 * cols, half), ordered[:, 1].reshape(2, 2 * cols, half)
    even_c = jnp.concatenate([re[0], re[0] * sign[0]]).astype(BF16)
    even_s = jnp.concatenate([-im[0], -im[0] * sign[0]]).astype(BF16)
    odd_c = jnp.concatenate([re[1], im[1] * sign[1]]).astype(BF16)
    odd_s = jnp.concatenate([-im[1], re[1] * sign[1]]).astype(BF16)
    dot = functools.partial(jnp.dot, preferred_element_type=F32)
    even = (dot(even_c, cos[0]) + dot(even_s, sin[0])).reshape(2, 2, cols, kpad)
    odd = (dot(odd_c, cos[1]) + dot(odd_s, sin[1])).reshape(2, 2, cols, kpad)
    even = jnp.where(second, even[:, 1], even[:, 0])
    odd = jnp.where(second, odd[:, 1], odd[:, 0])
    grid_values = jnp.stack(
        [even[0] + odd[0], even[1] - odd[1], even[0] - odd[0], even[1] + odd[1]], axis=1
    ).astype(BF16)
    grid_values = grid_values.reshape(cols, 4 * kpad)
    grid_values = lax.all_to_all(grid_values, "tile", split_axis=1, concat_axis=0, tiled=True)
    product = grid_products(grid_values)
    product = lax.all_to_all(product, "tile", split_axis=0, concat_axis=1, tiled=True)
    x = product.astype(F32).reshape(cols, 4, kpad)
    x = jnp.where(inside, x, 0.0)
    x0, x1, x2, x3 = x[:, 0], x[:, 1], x[:, 2], x[:, 3]
    def by_lat(a, b):
        both = jnp.stack([a, b])[:, None]
        return jnp.where(
            second == (lax.iota(jnp.int32, 2) == 1)[None, :, None, None], both, 0.0
        ).astype(BF16).reshape(4 * cols, kpad)
    even_in = by_lat((x0 + x2) + (x1 + x3), (x0 + x2) - (x1 + x3))
    odd_in = by_lat(x0 - x2, x1 - x3)
    nt = lambda a, b: lax.dot_general(
        a, b, (((1,), (1,)), ((), ())), preferred_element_type=F32
    ).reshape(2, 2, cols, half)
    ec, es = nt(even_in, cos[0]), nt(even_in, sin[0])
    oc, os_ = nt(odd_in, cos[1]), nt(odd_in, sin[1])
    pick = sign[0] > 0
    even_re = jnp.where(pick, ec[0], ec[1])
    even_im = -jnp.where(pick, es[0], es[1])
    odd_re = oc[0] - sign[1] * os_[1]
    odd_im = -os_[0] - sign[1] * oc[1]
    back = jnp.stack([jnp.stack([even_re, even_im]), jnp.stack([odd_re, odd_im])])
    back = back * jnp.where(keep, scales[None, :, None], 0.0)[:, None, :, None, :]
    back = back.astype(BF16).reshape(2, 2, 2, cols, 2, quarter_m).transpose(4, 2, 1, 3, 0, 5)
    back = back.reshape(2, 4 * cols, half)
    back = lax.dot_general(
        back, hot, (((2,), (2,)), ((0,), (0,))), preferred_element_type=F32
    ).astype(BF16)
    back = back.reshape(2, 2, 2 * cols, PAIRS).transpose(1, 0, 2, 3)
    returned = lax.all_to_all(back, "wave", split_axis=3, concat_axis=0, tiled=True)
    returned = returned.transpose(3, 2, 1, 0).reshape(slots, 2 * cols, 2 * lat_count)
    result = lax.dot_general(
        returned, masked, (((2,), (1,)), ((0,), (0,))), preferred_element_type=F32
    )
    return result.reshape(slots, 2, cols, row_total).astype(BF16)


def solution(mesh):
    placed = (P("wave", None, "tile", None), P("wave", None, None), P())
    return jax.shard_map(
        local, mesh=mesh, in_specs=placed, out_specs=P("wave", None, "tile", None), check_vma=False
    )
```

```python
import functools
import math

import jax
import jax.numpy as jnp
from jax import lax
from jax.experimental import pallas as pl
from jax.experimental.pallas import tpu as pltpu
from jax.sharding import PartitionSpec as P

MW = 1280
HALF_LATS = 1280
PAIRS = 640
NPTS = 5156
LANES = 128
RADIX = 32

F32 = jnp.float32
BF16 = jnp.bfloat16

HALF = MW // 2
GROUP = HALF // 2
GPAD = -(-GROUP // LANES) * LANES
BLOCKS = GPAD // RADIX
MESH = pl.DeviceIdType.MESH
NT = (((1,), (1,)), ((), ()))


def dot(a, b):
    return jnp.dot(a, b, preferred_element_type=F32)


def dot_nt(a, b):
    return lax.dot_general(a, b, NT, preferred_element_type=F32)


def middle_kernel(waves, tiles, cols, lat_count, kpad, *refs):
    (coef, ids, out, fx, gsend, grecv, psend, precv, bsend, cos_t, sin_t, small_c, small_s,
     hot, s1, r1, s2, r2, s3, r3, s4, r4) = refs
    wave, tile = lax.axis_index("wave"), lax.axis_index("tile")
    quarter = NPTS // 4
    halves = 4 * kpad // tiles
    per_d = tiles // 4
    rows = 2 * cols
    slots = coef.shape[2]

    def exchange(axis, here, count, src, dst, send, recv):
        copies = []
        for off in range(1, count):
            peer = lax.rem(here + off, count)
            copy = pltpu.make_async_remote_copy(
                src_ref=src.at[peer], dst_ref=dst.at[here], send_sem=send.at[off],
                recv_sem=recv.at[off], device_id={axis: peer}, device_id_type=MESH,
            )
            copy.start()
            copies.append(copy)
        dst[here] = src[here]
        return copies

    def finish(axis, here, count, src, dst, send, recv):
        for off in range(1, count):
            origin = lax.rem(here + count - off, count)
            pltpu.make_async_remote_copy(
                src_ref=src.at[origin], dst_ref=dst.at[origin], send_sem=send.at[off],
                recv_sem=recv.at[off], device_id={axis: origin}, device_id_type=MESH,
            ).wait_recv()

    barrier = pltpu.get_barrier_semaphore()
    for axis, here, count in (("wave", wave, waves), ("tile", tile, tiles)):
        for off in range(1, count):
            pl.semaphore_signal(
                barrier, inc=1, device_id={axis: lax.rem(here + off, count)}, device_id_type=MESH
            )
    pl.semaphore_wait(barrier, waves + tiles - 2)
    sends = exchange("wave", wave, waves, coef, fx, s1, r1)

    polar = wave * HALF // (lat_count // 2)
    q0 = 5 + polar
    n0, n1 = 4 * q0, NPTS - 4 * q0

    def line(shape, axis):
        return lax.broadcasted_iota(jnp.int32, shape, axis)

    k = line((1, kpad), 1)
    second = k >= q0
    inside = k < quarter
    point = jnp.where(inside, k - jnp.where(second, q0, 0), 0).astype(F32)
    length = jnp.where(second, n1, n0).astype(F32)

    def trig(m):
        whole = m.astype(F32) * point
        phase = whole - jnp.floor(whole / length) * length
        angle = (2.0 * math.pi) * phase / length
        return jnp.cos(angle), jnp.sin(angle)

    outer = 4 * BLOCKS
    r = line((outer, 1), 0)
    g, a = r // BLOCKS, r % BLOCKS
    c, s = trig((g // 2) * HALF + g % 2 + 2 * RADIX * a)
    small_c[0:outer] = c
    small_s[0:outer] = s
    c, s = trig(2 * line((RADIX, 1), 0))
    small_c[outer:] = c
    small_s[outer:] = s

    def block(idx, carry):
        ac, as_ = small_c[pl.ds(idx, 1), :], small_s[pl.ds(idx, 1), :]
        bc, bs = small_c[outer:, :], small_s[outer:, :]
        at = pl.ds(pl.multiple_of(idx * RADIX, RADIX), RADIX)
        cos_t[at, :] = (ac * bc - as_ * bs).astype(BF16)
        sin_t[at, :] = (as_ * bc + ac * bs).astype(BF16)
        return carry

    lax.fori_loop(0, outer, block, 0)

    lane = line((1, 2 * GPAD), 1)
    par = jnp.where(lane >= GPAD, 1, 0)
    i = lane - par * GPAD
    low = jnp.where(i < GROUP, 2 * i + par, -1)
    high = jnp.where(i < GROUP, HALF - 1 - par - 2 * i, -1)
    for w in range(waves):
        mine = ids[w]
        hot[0, w] = jnp.where(mine == low, 1.0, 0.0).astype(BF16)
        hot[1, w] = jnp.where(mine == high, 1.0, 0.0).astype(BF16)

    row = line((rows, 1), 0)
    n_row = jnp.where(row >= cols, n1, n0)
    cycle = jnp.where(row >= cols, HALF_LATS - 1 - polar, polar)
    weight = 40.0 * jnp.sin(math.pi * (cycle.astype(F32) + 0.5) / (2.0 * HALF_LATS))
    weight = weight / jnp.sqrt(lat_count * n_row.astype(F32))
    ii = line((1, GPAD), 1)
    up = ii % 2 == 0
    sign = jnp.where(up, 1.0, -1.0)

    def wavenumber(h, p):
        return h * HALF + p + 2 * ii

    def table(ref, h, p):
        start = (2 * h + p) * GPAD
        return ref[start : start + GPAD, :]

    finish("wave", wave, waves, coef, fx, s1, r1)
    even = jnp.zeros((2 * rows, kpad), F32)
    odd = jnp.zeros((2 * rows, kpad), F32)
    for h in range(2):
        both = jnp.zeros((2 * rows, 2 * GPAD), F32)
        for w in range(waves):
            both = both + dot(fx[w, h * 2 * rows : (h + 1) * 2 * rows, :], hot[h, w])
        for p in range(2):
            m = wavenumber(h, p)
            factor = jnp.where(2 * m < n_row, jnp.where(m == 0, 1.0, 2.0), 0.0)
            part = both[:, p * GPAD : (p + 1) * GPAD]
            re, im = part[:rows] * factor, part[rows:] * factor
            if p == 0:
                first = jnp.concatenate([re, re * sign]).astype(BF16)
                other = jnp.concatenate([-im, -im * sign]).astype(BF16)
                even = even + dot(first, table(cos_t, h, p)) + dot(other, table(sin_t, h, p))
            else:
                first = jnp.concatenate([re, im * sign]).astype(BF16)
                other = jnp.concatenate([-im, re * sign]).astype(BF16)
                odd = odd + dot(first, table(cos_t, h, p)) + dot(other, table(sin_t, h, p))

    def lat_of(x, v):
        return jnp.where(
            second, x[v * rows + cols : (v + 1) * rows], x[v * rows : v * rows + cols]
        )

    e0, e1, o0, o1 = lat_of(even, 0), lat_of(even, 1), lat_of(odd, 0), lat_of(odd, 1)
    for d, x in enumerate((e0 + o0, e1 - o1, e0 - o0, e1 + o1)):
        x = x.astype(BF16)
        for t in range(per_d):
            gsend[d * per_d + t] = x[:, t * halves : (t + 1) * halves]
    sends += exchange("tile", tile, tiles, gsend, grecv, s2, r2)
    finish("tile", tile, tiles, gsend, grecv, s2, r2)

    layers = cols * tiles // 4
    per_f = tiles // 4

    def field(f):
        return jnp.concatenate([grecv[f * per_f + t] for t in range(per_f)])

    u, w_, q = field(0).astype(F32), field(1).astype(F32), field(3).astype(F32)
    t16 = field(2)
    tri = jnp.where(line((layers, layers), 1) >= line((layers, layers), 0), 1.0, 0.0)
    geo = dot(tri.astype(BF16), t16) / math.sqrt(layers)
    temp = t16.astype(F32)
    for f, x in enumerate((0.5 * (u * u + w_ * w_) + geo, u * temp, w_ * temp, u * q)):
        x = x.astype(BF16)
        for t in range(per_f):
            psend[f * per_f + t] = x[t * cols : (t + 1) * cols]
    sends += exchange("tile", tile, tiles, psend, precv, s3, r3)
    finish("tile", tile, tiles, psend, precv, s3, r3)

    def quadrant(d):
        x = jnp.concatenate([precv[d * per_d + t].astype(F32) for t in range(per_d)], axis=1)
        return jnp.where(inside, x, 0.0)

    x0, x1, x2, x3 = [quadrant(d) for d in range(4)]

    def by_lat(*variants):
        return jnp.concatenate(
            [jnp.where(keep, v, 0.0) for v in variants for keep in (k < q0, second)]
        ).astype(BF16)

    even_in = by_lat((x0 + x2) + (x1 + x3), (x0 + x2) - (x1 + x3))
    odd_in = by_lat(x0 - x2, x1 - x3)
    for h in range(2):
        ec, es = dot_nt(even_in, table(cos_t, h, 0)), dot_nt(even_in, table(sin_t, h, 0))
        oc, os_ = dot_nt(odd_in, table(cos_t, h, 1)), dot_nt(odd_in, table(sin_t, h, 1))
        keep_e = jnp.where(2 * wavenumber(h, 0) < n_row, weight, 0.0)
        keep_o = jnp.where(2 * wavenumber(h, 1) < n_row, weight, 0.0)
        e_re = jnp.where(up, ec[:rows], ec[rows:]) * keep_e
        e_im = -jnp.where(up, es[:rows], es[rows:]) * keep_e
        o_re = (oc[:rows] - sign * os_[rows:]) * keep_o
        o_im = (-os_[:rows] - sign * oc[rows:]) * keep_o
        e_both = jnp.concatenate([e_re, e_im]).astype(BF16)
        o_both = jnp.concatenate([o_re, o_im]).astype(BF16)
        for w in range(waves):
            res = dot_nt(e_both, hot[h, w, :, :GPAD]) + dot_nt(o_both, hot[h, w, :, GPAD:])
            bsend[w, h * 2 * rows : (h + 1) * 2 * rows, :] = res.astype(BF16)
    sends += exchange("wave", wave, waves, bsend, out, s4, r4)
    finish("wave", wave, waves, bsend, out, s4, r4)
    for copy in sends:
        copy.wait_send()


def middle(coef, ids, waves, tiles, cols, lat_count):
    slots = coef.shape[2]
    step = max(tiles // 4, 1) * LANES
    kpad = -(-(NPTS // 4) // step) * step
    chunk = (tiles, cols, 4 * kpad // tiles)
    dma = pltpu.SemaphoreType.DMA
    vmem = pl.BlockSpec(memory_space=pltpu.VMEM)
    return pl.pallas_call(
        functools.partial(middle_kernel, waves, tiles, cols, lat_count, kpad),
        out_shape=jax.ShapeDtypeStruct(coef.shape, BF16),
        in_specs=[vmem, vmem],
        out_specs=vmem,
        scratch_shapes=[
            pltpu.VMEM(coef.shape, BF16),
            pltpu.VMEM(chunk, BF16), pltpu.VMEM(chunk, BF16),
            pltpu.VMEM(chunk, BF16), pltpu.VMEM(chunk, BF16),
            pltpu.VMEM(coef.shape, BF16),
            pltpu.VMEM((4 * GPAD, kpad), BF16), pltpu.VMEM((4 * GPAD, kpad), BF16),
            pltpu.VMEM((4 * BLOCKS + RADIX, kpad), F32),
            pltpu.VMEM((4 * BLOCKS + RADIX, kpad), F32),
            pltpu.VMEM((2, waves, slots, 2 * GPAD), BF16),
            dma((waves,)), dma((waves,)), dma((tiles,)), dma((tiles,)),
            dma((tiles,)), dma((tiles,)), dma((waves,)), dma((waves,)),
        ],
        compiler_params=pltpu.CompilerParams(
            collective_id=0, has_side_effects=True, vmem_limit_bytes=48 * 2**20
        ),
        name="middle",
    )(coef, ids)


def local(spectral, legendre, pair_ids):
    slots, _, cols, row_total = spectral.shape
    lat_count = legendre.shape[1]
    waves, tiles = lax.axis_size("wave"), lax.axis_size("tile")
    zero = jnp.zeros((), BF16)
    slot_ids = lax.dynamic_slice_in_dim(pair_ids, lax.axis_index("wave") * slots, slots)
    row_index = lax.broadcasted_iota(jnp.int32, (slots, row_total), 1)
    upper = (row_index >= (MW - slot_ids)[:, None])[:, None, :]
    masked = jnp.concatenate(
        [jnp.where(upper, zero, legendre), jnp.where(upper, legendre, zero)], axis=1
    )
    spec = spectral.reshape(slots, 2 * cols, row_total)
    coef = lax.dot_general(
        masked, spec, (((2,), (2,)), ((0,), (0,))), preferred_element_type=F32
    ).astype(BF16)
    coef = coef.reshape(slots, 2, waves, 2, 2, cols).transpose(2, 1, 4, 3, 5, 0)
    coef = coef.reshape(waves, 8 * cols, slots)
    back = middle(coef, pair_ids.reshape(waves, slots, 1), waves, tiles, cols, lat_count)
    back = back.reshape(waves, 2, 2, 2, cols, slots).transpose(5, 2, 4, 1, 0, 3)
    back = back.reshape(slots, 2 * cols, 2 * lat_count)
    result = lax.dot_general(
        back, masked, (((2,), (1,)), ((0,), (0,))), preferred_element_type=F32
    )
    return result.reshape(slots, 2, cols, row_total).astype(BF16)


def solution(mesh):
    placed = (P("wave", None, "tile", None), P("wave", None, None), P())
    return jax.shard_map(
        local, mesh=mesh, in_specs=placed, out_specs=P("wave", None, "tile", None), check_vma=False
    )
```

```python
import functools
import math

import jax
import jax.numpy as jnp
from jax import lax
from jax.experimental import pallas as pl
from jax.experimental.pallas import tpu as pltpu
from jax.sharding import PartitionSpec as P

MW = 1280
HALF_LATS = 1280
PAIRS = 640
NPTS = 5156
LANES = 128
RADIX = 32

F32 = jnp.float32
BF16 = jnp.bfloat16

HALF = MW // 2
GROUP = HALF // 2
GPAD = -(-GROUP // LANES) * LANES
BLOCKS = GPAD // RADIX
MESH = pl.DeviceIdType.MESH
NT = (((1,), (1,)), ((), ()))


def dot(a, b):
    return jnp.dot(a, b, preferred_element_type=F32)


def dot_nt(a, b):
    return lax.dot_general(a, b, NT, preferred_element_type=F32)


def middle_kernel(waves, tiles, cols, lat_count, kpad, *refs):
    (coef, ids, out, fx, gsend, grecv, psend, precv, bsend, cos_t, sin_t, small_c, small_s,
     hot, s1, r1, s2, r2, s3, r3, s4, r4) = refs
    wave, tile = lax.axis_index("wave"), lax.axis_index("tile")
    quarter = NPTS // 4
    halves = 4 * kpad // tiles
    per_d = tiles // 4
    rows = 2 * cols
    slots = coef.shape[2]

    def exchange(axis, here, count, src, dst, send, recv):
        copies = []
        for off in range(1, count):
            peer = lax.rem(here + off, count)
            copy = pltpu.make_async_remote_copy(
                src_ref=src.at[peer], dst_ref=dst.at[here], send_sem=send.at[off],
                recv_sem=recv.at[off], device_id={axis: peer}, device_id_type=MESH,
            )
            copy.start()
            copies.append(copy)
        dst[here] = src[here]
        return copies

    def finish(axis, here, count, src, dst, send, recv):
        for off in range(1, count):
            origin = lax.rem(here + count - off, count)
            pltpu.make_async_remote_copy(
                src_ref=src.at[origin], dst_ref=dst.at[origin], send_sem=send.at[off],
                recv_sem=recv.at[off], device_id={axis: origin}, device_id_type=MESH,
            ).wait_recv()

    barrier = pltpu.get_barrier_semaphore()
    for axis, here, count in (("wave", wave, waves), ("tile", tile, tiles)):
        for off in range(1, count):
            pl.semaphore_signal(
                barrier, inc=1, device_id={axis: lax.rem(here + off, count)}, device_id_type=MESH
            )
    pl.semaphore_wait(barrier, waves + tiles - 2)
    sends = exchange("wave", wave, waves, coef, fx, s1, r1)

    polar = wave * HALF // (lat_count // 2)
    q0 = 5 + polar
    n0, n1 = 4 * q0, NPTS - 4 * q0

    def line(shape, axis):
        return lax.broadcasted_iota(jnp.int32, shape, axis)

    k = line((1, kpad), 1)
    second = k >= q0
    inside = k < quarter
    point = jnp.where(inside, k - jnp.where(second, q0, 0), 0).astype(F32)
    length = jnp.where(second, n1, n0).astype(F32)

    def trig(m):
        whole = m.astype(F32) * point
        phase = whole - jnp.floor(whole / length) * length
        angle = (2.0 * math.pi) * phase / length
        return jnp.cos(angle), jnp.sin(angle)

    outer = 4 * BLOCKS
    r = line((outer, 1), 0)
    g, a = r // BLOCKS, r % BLOCKS
    c, s = trig((g // 2) * HALF + g % 2 + 2 * RADIX * a)
    small_c[0:outer] = c
    small_s[0:outer] = s
    c, s = trig(2 * line((RADIX, 1), 0))
    small_c[outer:] = c
    small_s[outer:] = s

    def block(idx, carry):
        ac, as_ = small_c[pl.ds(idx, 1), :], small_s[pl.ds(idx, 1), :]
        bc, bs = small_c[outer:, :], small_s[outer:, :]
        at = pl.ds(pl.multiple_of(idx * RADIX, RADIX), RADIX)
        cos_t[at, :] = (ac * bc - as_ * bs).astype(BF16)
        sin_t[at, :] = (as_ * bc + ac * bs).astype(BF16)
        return carry

    lax.fori_loop(0, outer, block, 0)

    lane = line((2 * GPAD, 1), 0)
    par = jnp.where(lane >= GPAD, 1, 0)
    i = lane - par * GPAD
    low = jnp.where(i < GROUP, 2 * i + par, -1)
    high = jnp.where(i < GROUP, HALF - 1 - par - 2 * i, -1)
    hot[0] = jnp.where(ids[...] == low, 1.0, 0.0).astype(BF16)
    hot[1] = jnp.where(ids[...] == high, 1.0, 0.0).astype(BF16)

    row = line((rows, 1), 0)
    n_row = jnp.where(row >= cols, n1, n0)
    cycle = jnp.where(row >= cols, HALF_LATS - 1 - polar, polar)
    weight = 40.0 * jnp.sin(math.pi * (cycle.astype(F32) + 0.5) / (2.0 * HALF_LATS))
    weight = weight / jnp.sqrt(lat_count * n_row.astype(F32))
    ii = line((1, GPAD), 1)
    up = ii % 2 == 0
    sign = jnp.where(up, 1.0, -1.0)

    def wavenumber(h, p):
        return h * HALF + p + 2 * ii

    def table(ref, h, p):
        start = (2 * h + p) * GPAD
        return ref[start : start + GPAD, :]

    finish("wave", wave, waves, coef, fx, s1, r1)
    even = jnp.zeros((2 * rows, kpad), F32)
    odd = jnp.zeros((2 * rows, kpad), F32)
    for h in range(2):
        here = [fx[w, h * 2 * rows : (h + 1) * 2 * rows, :] for w in range(waves)]
        both = dot_nt(jnp.concatenate(here, axis=1), hot[h])
        for p in range(2):
            m = wavenumber(h, p)
            factor = jnp.where(2 * m < n_row, jnp.where(m == 0, 1.0, 2.0), 0.0)
            part = both[:, p * GPAD : (p + 1) * GPAD]
            re, im = part[:rows] * factor, part[rows:] * factor
            if p == 0:
                first = jnp.concatenate([re, re * sign]).astype(BF16)
                other = jnp.concatenate([-im, -im * sign]).astype(BF16)
                even = even + dot(first, table(cos_t, h, p)) + dot(other, table(sin_t, h, p))
            else:
                first = jnp.concatenate([re, im * sign]).astype(BF16)
                other = jnp.concatenate([-im, re * sign]).astype(BF16)
                odd = odd + dot(first, table(cos_t, h, p)) + dot(other, table(sin_t, h, p))

    def lat_of(x, v):
        return jnp.where(
            second, x[v * rows + cols : (v + 1) * rows], x[v * rows : v * rows + cols]
        )

    e0, e1, o0, o1 = lat_of(even, 0), lat_of(even, 1), lat_of(odd, 0), lat_of(odd, 1)
    for d, x in enumerate((e0 + o0, e1 - o1, e0 - o0, e1 + o1)):
        x = x.astype(BF16)
        for t in range(per_d):
            gsend[d * per_d + t] = x[:, t * halves : (t + 1) * halves]
    sends += exchange("tile", tile, tiles, gsend, grecv, s2, r2)
    finish("tile", tile, tiles, gsend, grecv, s2, r2)

    layers = cols * tiles // 4
    per_f = tiles // 4

    def field(f):
        return jnp.concatenate([grecv[f * per_f + t] for t in range(per_f)])

    u, w_, q = field(0).astype(F32), field(1).astype(F32), field(3).astype(F32)
    t16 = field(2)
    tri = jnp.where(line((layers, layers), 1) >= line((layers, layers), 0), 1.0, 0.0)
    geo = dot(tri.astype(BF16), t16) / math.sqrt(layers)
    temp = t16.astype(F32)
    for f, x in enumerate((0.5 * (u * u + w_ * w_) + geo, u * temp, w_ * temp, u * q)):
        x = x.astype(BF16)
        for t in range(per_f):
            psend[f * per_f + t] = x[t * cols : (t + 1) * cols]
    sends += exchange("tile", tile, tiles, psend, precv, s3, r3)
    finish("tile", tile, tiles, psend, precv, s3, r3)

    def quadrant(d):
        x = jnp.concatenate([precv[d * per_d + t].astype(F32) for t in range(per_d)], axis=1)
        return jnp.where(inside, x, 0.0)

    x0, x1, x2, x3 = [quadrant(d) for d in range(4)]

    def by_lat(*variants):
        return jnp.concatenate(
            [jnp.where(keep, v, 0.0) for v in variants for keep in (k < q0, second)]
        ).astype(BF16)

    even_in = by_lat((x0 + x2) + (x1 + x3), (x0 + x2) - (x1 + x3))
    odd_in = by_lat(x0 - x2, x1 - x3)
    for h in range(2):
        ec, es = dot_nt(even_in, table(cos_t, h, 0)), dot_nt(even_in, table(sin_t, h, 0))
        oc, os_ = dot_nt(odd_in, table(cos_t, h, 1)), dot_nt(odd_in, table(sin_t, h, 1))
        keep_e = jnp.where(2 * wavenumber(h, 0) < n_row, weight, 0.0)
        keep_o = jnp.where(2 * wavenumber(h, 1) < n_row, weight, 0.0)
        e_re = jnp.where(up, ec[:rows], ec[rows:]) * keep_e
        e_im = -jnp.where(up, es[:rows], es[rows:]) * keep_e
        o_re = (oc[:rows] - sign * os_[rows:]) * keep_o
        o_im = (-os_[:rows] - sign * oc[rows:]) * keep_o
        e_both = jnp.concatenate([e_re, e_im]).astype(BF16)
        o_both = jnp.concatenate([o_re, o_im]).astype(BF16)
        res = (dot(e_both, hot[h, :GPAD]) + dot(o_both, hot[h, GPAD:])).astype(BF16)
        for w in range(waves):
            bsend[w, h * 2 * rows : (h + 1) * 2 * rows, :] = res[:, w * slots : (w + 1) * slots]
    sends += exchange("wave", wave, waves, bsend, out, s4, r4)
    finish("wave", wave, waves, bsend, out, s4, r4)
    for copy in sends:
        copy.wait_send()


def middle(coef, ids, waves, tiles, cols, lat_count):
    slots = coef.shape[2]
    step = max(tiles // 4, 1) * LANES
    kpad = -(-(NPTS // 4) // step) * step
    chunk = (tiles, cols, 4 * kpad // tiles)
    dma = pltpu.SemaphoreType.DMA
    vmem = pl.BlockSpec(memory_space=pltpu.VMEM)
    return pl.pallas_call(
        functools.partial(middle_kernel, waves, tiles, cols, lat_count, kpad),
        out_shape=jax.ShapeDtypeStruct(coef.shape, BF16),
        in_specs=[vmem, vmem],
        out_specs=vmem,
        scratch_shapes=[
            pltpu.VMEM(coef.shape, BF16),
            pltpu.VMEM(chunk, BF16), pltpu.VMEM(chunk, BF16),
            pltpu.VMEM(chunk, BF16), pltpu.VMEM(chunk, BF16),
            pltpu.VMEM(coef.shape, BF16),
            pltpu.VMEM((4 * GPAD, kpad), BF16), pltpu.VMEM((4 * GPAD, kpad), BF16),
            pltpu.VMEM((4 * BLOCKS + RADIX, kpad), F32),
            pltpu.VMEM((4 * BLOCKS + RADIX, kpad), F32),
            pltpu.VMEM((2, 2 * GPAD, waves * slots), BF16),
            dma((waves,)), dma((waves,)), dma((tiles,)), dma((tiles,)),
            dma((tiles,)), dma((tiles,)), dma((waves,)), dma((waves,)),
        ],
        compiler_params=pltpu.CompilerParams(
            collective_id=0, has_side_effects=True, vmem_limit_bytes=48 * 2**20
        ),
        name="middle",
    )(coef, ids)


def halves_of(ids, legendre, base, lane):
    parts = []
    for b in range(legendre.shape[0]):
        block = legendre[b]
        low = jnp.where(lane < MW - ids[base + b], 1.0, 0.0).astype(BF16) * block
        parts += [low, block - low]
    return jnp.concatenate(parts)


def same_slot(shape, rows, columns):
    row = lax.broadcasted_iota(jnp.int32, shape, 0) // rows
    return row == lax.broadcasted_iota(jnp.int32, shape, 1) // columns


def fold(rows, columns):
    row = lax.broadcasted_iota(jnp.int32, (rows, columns), 0) % columns
    same = row == lax.broadcasted_iota(jnp.int32, (rows, columns), 1)
    return jnp.where(same, 1.0, 0.0).astype(BF16)


def forward_kernel(slots, ids, spectral, legendre, out):
    take, lats, row_total = legendre.shape
    fields = spectral.shape[1] * spectral.shape[2]
    base = lax.axis_index("wave") * slots + pl.program_id(0) * take
    lane = lax.broadcasted_iota(jnp.int32, (1, row_total), 1)
    left = halves_of(ids, legendre, base, lane)
    right = spectral[...].reshape(take * fields, row_total)
    full = dot_nt(left, right)
    full = jnp.where(same_slot(full.shape, 2 * lats, fields), full, 0.0).astype(BF16)
    out[0] = dot(full, fold(take * fields, fields)).astype(BF16)


def inverse_kernel(slots, ids, back, legendre, out):
    take, lats, row_total = legendre.shape
    fields = out.shape[1] * out.shape[2]
    base = lax.axis_index("wave") * slots + pl.program_id(0) * take
    lane = lax.broadcasted_iota(jnp.int32, (1, row_total), 1)
    right = halves_of(ids, legendre, base, lane)
    wide = dot_nt(back[0], fold(take * 2 * lats, 2 * lats))
    wide = jnp.where(same_slot(wide.shape, fields, 2 * lats), wide, 0.0).astype(BF16)
    out[...] = dot(wide, right).astype(BF16).reshape(out.shape)


def local(spectral, legendre, pair_ids):
    slots, _, cols, row_total = spectral.shape
    lat_count = legendre.shape[1]
    waves, tiles = lax.axis_size("wave"), lax.axis_size("tile")
    take = max(b for b in range(1, 17) if slots % b == 0)
    groups = slots // take
    smem = pl.BlockSpec(memory_space=pltpu.SMEM)
    spec_block = pl.BlockSpec((take, 2, cols, row_total), lambda g: (g, 0, 0, 0))
    leg_block = pl.BlockSpec((take, lat_count, row_total), lambda g: (g, 0, 0))
    params = pltpu.CompilerParams(vmem_limit_bytes=40 * 2**20)
    coef = pl.pallas_call(
        functools.partial(forward_kernel, slots),
        grid=(groups,),
        out_shape=jax.ShapeDtypeStruct((groups, take * 2 * lat_count, 2 * cols), BF16),
        in_specs=[smem, spec_block, leg_block],
        out_specs=pl.BlockSpec((1, take * 2 * lat_count, 2 * cols), lambda g: (g, 0, 0)),
        compiler_params=params,
        name="forward",
    )(pair_ids, spectral, legendre)
    coef = coef.reshape(slots, 2, waves, 2, 2, cols).transpose(2, 1, 4, 3, 5, 0)
    coef = coef.reshape(waves, 8 * cols, slots)
    back = middle(coef, pair_ids.reshape(1, PAIRS), waves, tiles, cols, lat_count)
    back = back.reshape(waves, 2, 2, 2, cols, slots).transpose(5, 2, 4, 1, 0, 3)
    back = back.reshape(groups, take * 2 * cols, 2 * lat_count)
    return pl.pallas_call(
        functools.partial(inverse_kernel, slots),
        grid=(groups,),
        out_shape=jax.ShapeDtypeStruct(spectral.shape, BF16),
        in_specs=[
            smem,
            pl.BlockSpec((1, take * 2 * cols, 2 * lat_count), lambda g: (g, 0, 0)),
            leg_block,
        ],
        out_specs=spec_block,
        compiler_params=params,
        name="inverse",
    )(pair_ids, back, legendre)


def solution(mesh):
    placed = (P("wave", None, "tile", None), P("wave", None, None), P())
    return jax.shard_map(
        local, mesh=mesh, in_specs=placed, out_specs=P("wave", None, "tile", None), check_vma=False
    )
```

```python
import functools
import math

import jax
import jax.numpy as jnp
from jax import lax
from jax.experimental import pallas as pl
from jax.experimental.pallas import tpu as pltpu
from jax.sharding import PartitionSpec as P

MW = 1280
HALF_LATS = 1280
PAIRS = 640
NPTS = 5156
LANES = 128
RADIX = 32

F32 = jnp.float32
BF16 = jnp.bfloat16

HALF = MW // 2
GROUP = HALF // 2
GPAD = -(-GROUP // LANES) * LANES
BLOCKS = GPAD // RADIX
SPAN = 16
MESH = pl.DeviceIdType.MESH
NT = (((1,), (1,)), ((), ()))


def dot(a, b):
    return jnp.dot(a, b, preferred_element_type=F32)


def dot_nt(a, b):
    return lax.dot_general(a, b, NT, preferred_element_type=F32)


def middle_kernel(waves, tiles, cols, lat_count, kpad, *refs):
    (coef, ids, out, fx, gsend, grecv, psend, precv, bsend, trig_t, small_c, small_s, hot,
     s1, r1, s2, r2, s3, r3, s4, r4) = refs
    wave, tile = lax.axis_index("wave"), lax.axis_index("tile")
    quarter = NPTS // 4
    halves = 4 * kpad // tiles
    per_d = tiles // 4
    rows = 2 * cols
    slots = coef.shape[2]

    def exchange(axis, here, count, src, dst, send, recv):
        copies = []
        for off in range(1, count):
            peer = lax.rem(here + off, count)
            copy = pltpu.make_async_remote_copy(
                src_ref=src.at[peer], dst_ref=dst.at[here], send_sem=send.at[off],
                recv_sem=recv.at[off], device_id={axis: peer}, device_id_type=MESH,
            )
            copy.start()
            copies.append(copy)
        dst[here] = src[here]
        return copies

    def finish(axis, here, count, src, dst, send, recv):
        for off in range(1, count):
            origin = lax.rem(here + count - off, count)
            pltpu.make_async_remote_copy(
                src_ref=src.at[origin], dst_ref=dst.at[origin], send_sem=send.at[off],
                recv_sem=recv.at[off], device_id={axis: origin}, device_id_type=MESH,
            ).wait_recv()

    barrier = pltpu.get_barrier_semaphore()
    for axis, here, count in (("wave", wave, waves), ("tile", tile, tiles)):
        for off in range(1, count):
            pl.semaphore_signal(
                barrier, inc=1, device_id={axis: lax.rem(here + off, count)}, device_id_type=MESH
            )
    pl.semaphore_wait(barrier, waves + tiles - 2)
    sends = exchange("wave", wave, waves, coef, fx, s1, r1)

    polar = wave * HALF // (lat_count // 2)
    q0 = 5 + polar
    n0, n1 = 4 * q0, NPTS - 4 * q0

    def line(shape, axis):
        return lax.broadcasted_iota(jnp.int32, shape, axis)

    k = line((1, kpad), 1)
    second = k >= q0
    inside = k < quarter
    point = jnp.where(inside, k - jnp.where(second, q0, 0), 0).astype(F32)
    length = jnp.where(second, n1, n0).astype(F32)

    def trig(m):
        whole = m.astype(F32) * point
        phase = whole - jnp.floor(whole / length) * length
        angle = (2.0 * math.pi) * phase / length
        return jnp.cos(angle), jnp.sin(angle)

    r = line((RADIX, 1), 0)
    m = jnp.where(r < 8, 2 * r, 16 * (r - 8))
    m = jnp.where(r >= 12, (r - 12) // 2 * HALF + (r - 12) % 2, m)
    m = jnp.where(r >= 16, 2 * RADIX * (r - 16), m)
    c, s = trig(m)
    outer = 4 * SPAN
    for g in range(4):
        ca, sa, cb, sb = c[16:], s[16:], c[12 + g : 13 + g], s[12 + g : 13 + g]
        small_c[g * SPAN : (g + 1) * SPAN] = ca * cb - sa * sb
        small_s[g * SPAN : (g + 1) * SPAN] = sa * cb + ca * sb
        ca, sa, cb, sb = c[:8], s[:8], c[8 + g : 9 + g], s[8 + g : 9 + g]
        small_c[outer + 8 * g : outer + 8 * g + 8] = ca * cb - sa * sb
        small_s[outer + 8 * g : outer + 8 * g + 8] = sa * cb + ca * sb

    def block(idx, carry):
        g, a = idx // BLOCKS, idx % BLOCKS
        row_a = g * SPAN + a
        ac, as_ = small_c[pl.ds(row_a, 1), :], small_s[pl.ds(row_a, 1), :]
        bc, bs = small_c[outer:, :], small_s[outer:, :]
        at = ((g % 2) * 4 + g // 2) * GPAD + a * RADIX
        cos_at = pl.ds(pl.multiple_of(at, RADIX), RADIX)
        sin_at = pl.ds(pl.multiple_of(at + 2 * GPAD, RADIX), RADIX)
        trig_t[cos_at, :] = (ac * bc - as_ * bs).astype(BF16)
        trig_t[sin_at, :] = (as_ * bc + ac * bs).astype(BF16)
        return carry

    lax.fori_loop(0, 4 * BLOCKS, block, 0)

    lane = line((2 * GPAD, 1), 0)
    par = jnp.where(lane >= GPAD, 1, 0)
    i = lane - par * GPAD
    low = jnp.where(i < GROUP, 2 * i + par, -1)
    high = jnp.where(i < GROUP, HALF - 1 - par - 2 * i, -1)
    pair = ids[...].reshape(1, ids.shape[0])
    hot[0] = jnp.where(pair == low, 1.0, 0.0).astype(BF16)
    hot[1] = jnp.where(pair == high, 1.0, 0.0).astype(BF16)

    row = line((rows, 1), 0)
    n_row = jnp.where(row >= cols, n1, n0)
    cycle = jnp.where(row >= cols, HALF_LATS - 1 - polar, polar)
    weight = 40.0 * jnp.sin(math.pi * (cycle.astype(F32) + 0.5) / (2.0 * HALF_LATS))
    weight = weight / jnp.sqrt(lat_count * n_row.astype(F32))
    ii = line((1, GPAD), 1)
    up = ii % 2 == 0
    sign = jnp.where(up, 1.0, -1.0)

    def wavenumber(h, p):
        return h * HALF + p + 2 * ii

    def table(p):
        return trig_t[p * 4 * GPAD : (p + 1) * 4 * GPAD, :]

    finish("wave", wave, waves, coef, fx, s1, r1)
    terms = [[[], []], [[], []]]
    for h in range(2):
        here = [fx[w, h * 2 * rows : (h + 1) * 2 * rows, :] for w in range(waves)]
        both = dot_nt(jnp.concatenate(here, axis=1), hot[h])
        for p in range(2):
            m = wavenumber(h, p)
            factor = jnp.where(2 * m < n_row, jnp.where(m == 0, 1.0, 2.0), 0.0)
            part = both[:, p * GPAD : (p + 1) * GPAD]
            re, im = part[:rows] * factor, part[rows:] * factor
            cos_side, sin_side = ((re, re), (-im, -im)) if p == 0 else ((re, im), (-im, re))
            for x, (a, b) in enumerate((cos_side, sin_side)):
                terms[p][x].append(jnp.concatenate([a, b * sign]).astype(BF16))
    even = dot(jnp.concatenate(terms[0][0] + terms[0][1], axis=1), table(0))
    odd = dot(jnp.concatenate(terms[1][0] + terms[1][1], axis=1), table(1))

    def lat_of(x, v):
        return jnp.where(
            second, x[v * rows + cols : (v + 1) * rows], x[v * rows : v * rows + cols]
        )

    e0, e1, o0, o1 = lat_of(even, 0), lat_of(even, 1), lat_of(odd, 0), lat_of(odd, 1)
    for d, x in enumerate((e0 + o0, e1 - o1, e0 - o0, e1 + o1)):
        x = x.astype(BF16)
        for t in range(per_d):
            gsend[d * per_d + t] = x[:, t * halves : (t + 1) * halves]
    sends += exchange("tile", tile, tiles, gsend, grecv, s2, r2)
    finish("tile", tile, tiles, gsend, grecv, s2, r2)

    layers = cols * tiles // 4
    per_f = tiles // 4

    def field(f):
        return jnp.concatenate([grecv[f * per_f + t] for t in range(per_f)])

    u, w_, q = field(0).astype(F32), field(1).astype(F32), field(3).astype(F32)
    t16 = field(2)
    tri = jnp.where(line((layers, layers), 1) >= line((layers, layers), 0), 1.0, 0.0)
    geo = dot(tri.astype(BF16), t16) / math.sqrt(layers)
    temp = t16.astype(F32)
    for f, x in enumerate((0.5 * (u * u + w_ * w_) + geo, u * temp, w_ * temp, u * q)):
        x = x.astype(BF16)
        for t in range(per_f):
            psend[f * per_f + t] = x[t * cols : (t + 1) * cols]
    sends += exchange("tile", tile, tiles, psend, precv, s3, r3)
    finish("tile", tile, tiles, psend, precv, s3, r3)

    def quadrant(d):
        x = jnp.concatenate([precv[d * per_d + t].astype(F32) for t in range(per_d)], axis=1)
        return jnp.where(inside, x, 0.0)

    x0, x1, x2, x3 = [quadrant(d) for d in range(4)]

    def by_lat(*variants):
        return jnp.concatenate(
            [jnp.where(keep, v, 0.0) for v in variants for keep in (k < q0, second)]
        ).astype(BF16)

    even_in = by_lat((x0 + x2) + (x1 + x3), (x0 + x2) - (x1 + x3))
    odd_in = by_lat(x0 - x2, x1 - x3)
    even_out, odd_out = dot_nt(even_in, table(0)), dot_nt(odd_in, table(1))
    for h in range(2):
        at_c, at_s = slice(h * GPAD, (h + 1) * GPAD), slice((2 + h) * GPAD, (3 + h) * GPAD)
        ec, es, oc, os_ = even_out[:, at_c], even_out[:, at_s], odd_out[:, at_c], odd_out[:, at_s]
        keep_e = jnp.where(2 * wavenumber(h, 0) < n_row, weight, 0.0)
        keep_o = jnp.where(2 * wavenumber(h, 1) < n_row, weight, 0.0)
        e_re = jnp.where(up, ec[:rows], ec[rows:]) * keep_e
        e_im = -jnp.where(up, es[:rows], es[rows:]) * keep_e
        o_re = (oc[:rows] - sign * os_[rows:]) * keep_o
        o_im = (-os_[:rows] - sign * oc[rows:]) * keep_o
        e_both = jnp.concatenate([e_re, e_im]).astype(BF16)
        o_both = jnp.concatenate([o_re, o_im]).astype(BF16)
        res = (dot(e_both, hot[h, :GPAD]) + dot(o_both, hot[h, GPAD:])).astype(BF16)
        for w in range(waves):
            bsend[w, h * 2 * rows : (h + 1) * 2 * rows, :] = res[:, w * slots : (w + 1) * slots]
    sends += exchange("wave", wave, waves, bsend, out, s4, r4)
    finish("wave", wave, waves, bsend, out, s4, r4)
    for copy in sends:
        copy.wait_send()


def middle(coef, ids, waves, tiles, cols, lat_count):
    slots = coef.shape[2]
    step = max(tiles // 4, 1) * LANES
    kpad = -(-(NPTS // 4) // step) * step
    chunk = (tiles, cols, 4 * kpad // tiles)
    dma = pltpu.SemaphoreType.DMA
    vmem = pl.BlockSpec(memory_space=pltpu.VMEM)
    return pl.pallas_call(
        functools.partial(middle_kernel, waves, tiles, cols, lat_count, kpad),
        out_shape=jax.ShapeDtypeStruct(coef.shape, BF16),
        in_specs=[vmem, vmem],
        out_specs=vmem,
        scratch_shapes=[
            pltpu.VMEM(coef.shape, BF16),
            pltpu.VMEM(chunk, BF16), pltpu.VMEM(chunk, BF16),
            pltpu.VMEM(chunk, BF16), pltpu.VMEM(chunk, BF16),
            pltpu.VMEM(coef.shape, BF16),
            pltpu.VMEM((8 * GPAD, kpad), BF16),
            pltpu.VMEM((4 * SPAN + RADIX, kpad), F32),
            pltpu.VMEM((4 * SPAN + RADIX, kpad), F32),
            pltpu.VMEM((2, 2 * GPAD, waves * slots), BF16),
            dma((waves,)), dma((waves,)), dma((tiles,)), dma((tiles,)),
            dma((tiles,)), dma((tiles,)), dma((waves,)), dma((waves,)),
        ],
        compiler_params=pltpu.CompilerParams(
            collective_id=0, has_side_effects=True, vmem_limit_bytes=60 * 2**20
        ),
        name="middle",
    )(coef, ids)


def halves_of(ids, legendre, base, lane):
    parts = []
    for b in range(legendre.shape[0]):
        block = legendre[b].astype(F32)
        low = lane < MW - ids[base + b]
        both = [jnp.where(low, block, 0.0), jnp.where(low, 0.0, block)]
        parts.append(jnp.concatenate(both).astype(BF16))
    return jnp.concatenate(parts)


def same_slot(shape, rows, columns):
    row = lax.broadcasted_iota(jnp.int32, shape, 0) // rows
    return row == lax.broadcasted_iota(jnp.int32, shape, 1) // columns


def fold(rows, columns):
    row = lax.broadcasted_iota(jnp.int32, (rows, columns), 0) % columns
    same = row == lax.broadcasted_iota(jnp.int32, (rows, columns), 1)
    return jnp.where(same, 1.0, 0.0).astype(BF16)


def forward_kernel(slots, ids, spectral, legendre, out):
    take, lats, row_total = legendre.shape
    fields = spectral.shape[1] * spectral.shape[2]
    base = lax.axis_index("wave") * slots + pl.program_id(0) * take
    lane = lax.broadcasted_iota(jnp.int32, (lats, row_total), 1)
    left = halves_of(ids, legendre, base, lane)
    right = spectral[...].astype(F32).reshape(take * fields, row_total).astype(BF16)
    full = dot_nt(left, right)
    full = jnp.where(same_slot(full.shape, 2 * lats, fields), full, 0.0).astype(BF16)
    out[...] = dot(full, fold(take * fields, fields)).astype(BF16).reshape(out.shape)


def inverse_kernel(slots, ids, back, legendre, out):
    take, lats, row_total = legendre.shape
    fields = out.shape[1] * out.shape[2]
    base = lax.axis_index("wave") * slots + pl.program_id(0) * take
    lane = lax.broadcasted_iota(jnp.int32, (lats, row_total), 1)
    right = halves_of(ids, legendre, base, lane)
    narrow = back[...].reshape(take * fields, 2 * lats)
    wide = dot_nt(narrow, fold(take * 2 * lats, 2 * lats))
    wide = jnp.where(same_slot(wide.shape, fields, 2 * lats), wide, 0.0).astype(BF16)
    out[...] = dot(wide, right).reshape(out.shape).astype(BF16)


def local(spectral, legendre, pair_ids):
    slots, _, cols, row_total = spectral.shape
    lat_count = legendre.shape[1]
    waves, tiles = lax.axis_size("wave"), lax.axis_size("tile")
    take = max(b for b in range(1, 17) if slots % b == 0)
    groups = slots // take
    smem = pl.BlockSpec(memory_space=pltpu.SMEM)
    spec_block = pl.BlockSpec((take, 2, cols, row_total), lambda g: (g, 0, 0, 0))
    leg_block = pl.BlockSpec((take, lat_count, row_total), lambda g: (g, 0, 0))
    params = pltpu.CompilerParams(vmem_limit_bytes=60 * 2**20)
    coef = pl.pallas_call(
        functools.partial(forward_kernel, slots),
        grid=(groups,),
        out_shape=jax.ShapeDtypeStruct((slots, 2 * lat_count, 2 * cols), BF16),
        in_specs=[smem, spec_block, leg_block],
        out_specs=pl.BlockSpec((take, 2 * lat_count, 2 * cols), lambda g: (g, 0, 0)),
        compiler_params=params,
        name="forward",
    )(pair_ids, spectral, legendre)
    coef = coef.reshape(slots, 2, waves, 2, 2, cols).transpose(2, 1, 4, 3, 5, 0)
    coef = coef.reshape(waves, 8 * cols, slots)
    back = middle(coef, pair_ids, waves, tiles, cols, lat_count)
    back = back.reshape(waves, 2, 2, 2, cols, slots).transpose(5, 2, 4, 1, 0, 3)
    back = back.reshape(slots, 2 * cols, 2 * lat_count)
    return pl.pallas_call(
        functools.partial(inverse_kernel, slots),
        grid=(groups,),
        out_shape=jax.ShapeDtypeStruct(spectral.shape, BF16),
        in_specs=[
            smem,
            pl.BlockSpec((take, 2 * cols, 2 * lat_count), lambda g: (g, 0, 0)),
            leg_block,
        ],
        out_specs=spec_block,
        compiler_params=params,
        name="inverse",
    )(pair_ids, back, legendre)


def solution(mesh):
    placed = (P("wave", None, "tile", None), P("wave", None, None), P())
    return jax.shard_map(
        local, mesh=mesh, in_specs=placed, out_specs=P("wave", None, "tile", None), check_vma=False
    )
```

```python
import functools
import math

import jax
import jax.numpy as jnp
from jax import lax
from jax.experimental import pallas as pl
from jax.experimental.pallas import tpu as pltpu
from jax.sharding import PartitionSpec as P

MW = 1280
HALF_LATS = 1280
PAIRS = 640
NPTS = 5156
LANES = 128
RADIX = 32

F32 = jnp.float32
BF16 = jnp.bfloat16

HALF = MW // 2
GROUP = HALF // 2
GPAD = -(-GROUP // LANES) * LANES
BLOCKS = GPAD // RADIX
SPAN = 16
MESH = pl.DeviceIdType.MESH
NT = (((1,), (1,)), ((), ()))


def dot(a, b):
    return jnp.dot(a, b, preferred_element_type=F32)


def dot_nt(a, b):
    return lax.dot_general(a, b, NT, preferred_element_type=F32)


def middle_kernel(waves, tiles, cols, lat_count, kpad, *refs):
    (coef, ids, out, fx, gsend, grecv, psend, precv, bsend, trig_t, small_c, small_s, hot,
     s1, r1, s2, r2, s3, r3, s4, r4) = refs
    wave, tile = lax.axis_index("wave"), lax.axis_index("tile")
    quarter = NPTS // 4
    halves = 4 * kpad // tiles
    per_d = tiles // 4
    rows = 2 * cols
    slots = coef.shape[2]

    def exchange(axis, here, count, src, dst, send, recv):
        copies = []
        for off in range(1, count):
            peer = lax.rem(here + off, count)
            copy = pltpu.make_async_remote_copy(
                src_ref=src.at[peer], dst_ref=dst.at[here], send_sem=send.at[off],
                recv_sem=recv.at[off], device_id={axis: peer}, device_id_type=MESH,
            )
            copy.start()
            copies.append(copy)
        dst[here] = src[here]
        return copies

    def finish(axis, here, count, src, dst, send, recv):
        for off in range(1, count):
            origin = lax.rem(here + count - off, count)
            pltpu.make_async_remote_copy(
                src_ref=src.at[origin], dst_ref=dst.at[origin], send_sem=send.at[off],
                recv_sem=recv.at[off], device_id={axis: origin}, device_id_type=MESH,
            ).wait_recv()

    barrier = pltpu.get_barrier_semaphore()
    for axis, here, count in (("wave", wave, waves), ("tile", tile, tiles)):
        for off in range(1, count):
            pl.semaphore_signal(
                barrier, inc=1, device_id={axis: lax.rem(here + off, count)}, device_id_type=MESH
            )
    pl.semaphore_wait(barrier, waves + tiles - 2)
    sends = exchange("wave", wave, waves, coef, fx, s1, r1)

    polar = wave * HALF // (lat_count // 2)
    q0 = 5 + polar
    n0, n1 = 4 * q0, NPTS - 4 * q0

    def line(shape, axis):
        return lax.broadcasted_iota(jnp.int32, shape, axis)

    k = line((1, kpad), 1)
    second = k >= q0
    inside = k < quarter
    point = jnp.where(inside, k - jnp.where(second, q0, 0), 0).astype(F32)
    length = jnp.where(second, n1, n0).astype(F32)

    def trig(m):
        whole = m.astype(F32) * point
        phase = whole - jnp.floor(whole / length) * length
        angle = (2.0 * math.pi) * phase / length
        return jnp.cos(angle), jnp.sin(angle)

    r = line((RADIX, 1), 0)
    m = jnp.where(r < 8, 2 * r, 16 * (r - 8))
    m = jnp.where(r >= 12, (r - 12) // 2 * HALF + (r - 12) % 2, m)
    m = jnp.where(r >= 16, 2 * RADIX * (r - 16), m)
    c, s = trig(m)
    outer = 4 * SPAN
    for g in range(4):
        ca, sa, cb, sb = c[16:], s[16:], c[12 + g : 13 + g], s[12 + g : 13 + g]
        small_c[g * SPAN : (g + 1) * SPAN] = ca * cb - sa * sb
        small_s[g * SPAN : (g + 1) * SPAN] = sa * cb + ca * sb
        ca, sa, cb, sb = c[:8], s[:8], c[8 + g : 9 + g], s[8 + g : 9 + g]
        small_c[outer + 8 * g : outer + 8 * g + 8] = ca * cb - sa * sb
        small_s[outer + 8 * g : outer + 8 * g + 8] = sa * cb + ca * sb

    def block(idx, carry):
        g, a = idx // BLOCKS, idx % BLOCKS
        row_a = g * SPAN + a
        ac, as_ = small_c[pl.ds(row_a, 1), :], small_s[pl.ds(row_a, 1), :]
        bc, bs = small_c[outer:, :], small_s[outer:, :]
        at = ((g % 2) * 4 + g // 2) * GPAD + a * RADIX
        cos_at = pl.ds(pl.multiple_of(at, RADIX), RADIX)
        sin_at = pl.ds(pl.multiple_of(at + 2 * GPAD, RADIX), RADIX)
        trig_t[cos_at, :] = (ac * bc - as_ * bs).astype(BF16)
        trig_t[sin_at, :] = (as_ * bc + ac * bs).astype(BF16)
        return carry

    lax.fori_loop(0, 4 * BLOCKS, block, 0)

    lane = line((2 * GPAD, 1), 0)
    par = jnp.where(lane >= GPAD, 1, 0)
    i = lane - par * GPAD
    low = jnp.where(i < GROUP, 2 * i + par, -1)
    high = jnp.where(i < GROUP, HALF - 1 - par - 2 * i, -1)
    pair = ids[...].reshape(1, ids.shape[0])
    hot[0] = jnp.where(pair == low, 1.0, 0.0).astype(BF16)
    hot[1] = jnp.where(pair == high, 1.0, 0.0).astype(BF16)

    row = line((rows, 1), 0)
    n_row = jnp.where(row >= cols, n1, n0)
    cycle = jnp.where(row >= cols, HALF_LATS - 1 - polar, polar)
    weight = 40.0 * jnp.sin(math.pi * (cycle.astype(F32) + 0.5) / (2.0 * HALF_LATS))
    weight = weight / jnp.sqrt(lat_count * n_row.astype(F32))
    ii = line((1, GPAD), 1)
    up = ii % 2 == 0
    sign = jnp.where(up, 1.0, -1.0)

    def wavenumber(h, p):
        return h * HALF + p + 2 * ii

    def table(p):
        return trig_t[p * 4 * GPAD : (p + 1) * 4 * GPAD, :]

    finish("wave", wave, waves, coef, fx, s1, r1)
    terms = [[[], []], [[], []]]
    for h in range(2):
        here = [fx[w, h * 2 * rows : (h + 1) * 2 * rows, :] for w in range(waves)]
        both = dot_nt(jnp.concatenate(here, axis=1), hot[h])
        for p in range(2):
            m = wavenumber(h, p)
            factor = jnp.where(2 * m < n_row, jnp.where(m == 0, 1.0, 2.0), 0.0)
            part = both[:, p * GPAD : (p + 1) * GPAD]
            re, im = part[:rows] * factor, part[rows:] * factor
            cos_side, sin_side = ((re, re), (-im, -im)) if p == 0 else ((re, im), (-im, re))
            for x, (a, b) in enumerate((cos_side, sin_side)):
                terms[p][x].append(jnp.concatenate([a, b * sign]).astype(BF16))
    even = dot(jnp.concatenate(terms[0][0] + terms[0][1], axis=1), table(0))
    odd = dot(jnp.concatenate(terms[1][0] + terms[1][1], axis=1), table(1))

    def lat_of(x, v):
        return jnp.where(
            second, x[v * rows + cols : (v + 1) * rows], x[v * rows : v * rows + cols]
        )

    e0, e1, o0, o1 = lat_of(even, 0), lat_of(even, 1), lat_of(odd, 0), lat_of(odd, 1)
    for d, x in enumerate((e0 + o0, e1 - o1, e0 - o0, e1 + o1)):
        x = x.astype(BF16)
        for t in range(per_d):
            gsend[d * per_d + t] = x[:, t * halves : (t + 1) * halves]
    sends += exchange("tile", tile, tiles, gsend, grecv, s2, r2)
    finish("tile", tile, tiles, gsend, grecv, s2, r2)

    layers = cols * tiles // 4
    per_f = tiles // 4

    def field(f):
        return jnp.concatenate([grecv[f * per_f + t] for t in range(per_f)])

    u, w_, q = field(0).astype(F32), field(1).astype(F32), field(3).astype(F32)
    t16 = field(2)
    tri = jnp.where(line((layers, layers), 1) >= line((layers, layers), 0), 1.0, 0.0)
    geo = dot(tri.astype(BF16), t16) / math.sqrt(layers)
    temp = t16.astype(F32)
    for f, x in enumerate((0.5 * (u * u + w_ * w_) + geo, u * temp, w_ * temp, u * q)):
        x = x.astype(BF16)
        for t in range(per_f):
            psend[f * per_f + t] = x[t * cols : (t + 1) * cols]
    sends += exchange("tile", tile, tiles, psend, precv, s3, r3)
    finish("tile", tile, tiles, psend, precv, s3, r3)

    def quadrant(d):
        x = jnp.concatenate([precv[d * per_d + t].astype(F32) for t in range(per_d)], axis=1)
        return jnp.where(inside, x, 0.0)

    x0, x1, x2, x3 = [quadrant(d) for d in range(4)]

    def by_lat(*variants):
        return jnp.concatenate(
            [jnp.where(keep, v, 0.0) for v in variants for keep in (k < q0, second)]
        ).astype(BF16)

    even_in = by_lat((x0 + x2) + (x1 + x3), (x0 + x2) - (x1 + x3))
    odd_in = by_lat(x0 - x2, x1 - x3)
    even_out, odd_out = dot_nt(even_in, table(0)), dot_nt(odd_in, table(1))
    for h in range(2):
        at_c, at_s = slice(h * GPAD, (h + 1) * GPAD), slice((2 + h) * GPAD, (3 + h) * GPAD)
        ec, es, oc, os_ = even_out[:, at_c], even_out[:, at_s], odd_out[:, at_c], odd_out[:, at_s]
        keep_e = jnp.where(2 * wavenumber(h, 0) < n_row, weight, 0.0)
        keep_o = jnp.where(2 * wavenumber(h, 1) < n_row, weight, 0.0)
        e_re = jnp.where(up, ec[:rows], ec[rows:]) * keep_e
        e_im = -jnp.where(up, es[:rows], es[rows:]) * keep_e
        o_re = (oc[:rows] - sign * os_[rows:]) * keep_o
        o_im = (-os_[:rows] - sign * oc[rows:]) * keep_o
        e_both = jnp.concatenate([e_re, e_im]).astype(BF16)
        o_both = jnp.concatenate([o_re, o_im]).astype(BF16)
        res = (dot(e_both, hot[h, :GPAD]) + dot(o_both, hot[h, GPAD:])).astype(BF16)
        for w in range(waves):
            bsend[w, h * 2 * rows : (h + 1) * 2 * rows, :] = res[:, w * slots : (w + 1) * slots]
    sends += exchange("wave", wave, waves, bsend, out, s4, r4)
    finish("wave", wave, waves, bsend, out, s4, r4)
    for copy in sends:
        copy.wait_send()


def middle(coef, ids, waves, tiles, cols, lat_count):
    slots = coef.shape[2]
    step = max(tiles // 4, 1) * LANES
    kpad = -(-(NPTS // 4) // step) * step
    chunk = (tiles, cols, 4 * kpad // tiles)
    dma = pltpu.SemaphoreType.DMA
    vmem = pl.BlockSpec(memory_space=pltpu.VMEM)
    return pl.pallas_call(
        functools.partial(middle_kernel, waves, tiles, cols, lat_count, kpad),
        out_shape=jax.ShapeDtypeStruct(coef.shape, BF16),
        in_specs=[vmem, vmem],
        out_specs=vmem,
        scratch_shapes=[
            pltpu.VMEM(coef.shape, BF16),
            pltpu.VMEM(chunk, BF16), pltpu.VMEM(chunk, BF16),
            pltpu.VMEM(chunk, BF16), pltpu.VMEM(chunk, BF16),
            pltpu.VMEM(coef.shape, BF16),
            pltpu.VMEM((8 * GPAD, kpad), BF16),
            pltpu.VMEM((4 * SPAN + RADIX, kpad), F32),
            pltpu.VMEM((4 * SPAN + RADIX, kpad), F32),
            pltpu.VMEM((2, 2 * GPAD, waves * slots), BF16),
            dma((waves,)), dma((waves,)), dma((tiles,)), dma((tiles,)),
            dma((tiles,)), dma((tiles,)), dma((waves,)), dma((waves,)),
        ],
        compiler_params=pltpu.CompilerParams(
            collective_id=0, has_side_effects=True, vmem_limit_bytes=40 * 2**20
        ),
        name="middle",
    )(coef, ids)


def halves_of(ids, block, base):
    lane = lax.broadcasted_iota(jnp.int32, block.shape[1:], 1)
    parts = []
    for b in range(block.shape[0]):
        rows = block[b].astype(F32)
        low = lane < MW - ids[base + b]
        both = [jnp.where(low, rows, 0.0), jnp.where(low, 0.0, rows)]
        parts.append(jnp.concatenate(both).astype(BF16))
    return jnp.concatenate(parts)


def same_slot(shape, rows, columns):
    row = lax.broadcasted_iota(jnp.int32, shape, 0) // rows
    return row == lax.broadcasted_iota(jnp.int32, shape, 1) // columns


def fold(rows, columns):
    row = lax.broadcasted_iota(jnp.int32, (rows, columns), 0) % columns
    same = row == lax.broadcasted_iota(jnp.int32, (rows, columns), 1)
    return jnp.where(same, 1.0, 0.0).astype(BF16)


def forward_kernel(take, ids, spectral, legendre, out, spec_v, leg_v, spec_sem, leg_sem):
    slots, lats, row_total = legendre.shape
    fields = spectral.shape[1] * spectral.shape[2]
    base = lax.axis_index("wave") * slots
    copies = []
    for g in range(slots // take):
        at = pl.ds(g * take, take)
        pair = [
            pltpu.make_async_copy(legendre.at[at], leg_v.at[at], leg_sem.at[g]),
            pltpu.make_async_copy(spectral.at[at], spec_v.at[at], spec_sem.at[g]),
        ]
        for copy in pair:
            copy.start()
        copies.append(pair)
    shape = (take * 2 * lats, take * fields)
    same = same_slot(shape, 2 * lats, fields)
    folded = fold(take * fields, fields)
    for g, pair in enumerate(copies):
        for copy in pair:
            copy.wait()
        here = slice(g * take, (g + 1) * take)
        left = halves_of(ids, leg_v[here], base + g * take)
        right = spec_v[here].astype(F32).reshape(take * fields, row_total).astype(BF16)
        full = jnp.where(same, dot_nt(left, right), 0.0).astype(BF16)
        full = dot(full, folded).astype(BF16)
        out[here] = full.reshape((take,) + out.shape[1:])


def inverse_kernel(take, ids, back, legendre, out, leg_v, out_v, leg_sem, out_sem):
    slots, lats, row_total = legendre.shape
    fields = out.shape[1] * out.shape[2]
    base = lax.axis_index("wave") * slots
    copies = []
    for g in range(slots // take):
        at = pl.ds(g * take, take)
        copies.append(pltpu.make_async_copy(legendre.at[at], leg_v.at[at], leg_sem.at[g]))
        copies[-1].start()
    shape = (take * fields, take * 2 * lats)
    same = same_slot(shape, fields, 2 * lats)
    folded = fold(take * 2 * lats, 2 * lats)
    results = []
    for g, copy in enumerate(copies):
        at = pl.ds(g * take, take)
        here = slice(g * take, (g + 1) * take)
        narrow = back[here].reshape(take * fields, 2 * lats)
        wide = jnp.where(same, dot_nt(narrow, folded), 0.0).astype(BF16)
        copy.wait()
        right = halves_of(ids, leg_v[here], base + g * take)
        out_v[here] = dot(wide, right).reshape((take,) + out.shape[1:]).astype(BF16)
        results.append(pltpu.make_async_copy(out_v.at[at], out.at[at], out_sem.at[g]))
        results[-1].start()
    for copy in results:
        copy.wait()


def local(spectral, legendre, pair_ids):
    slots, _, cols, row_total = spectral.shape
    lat_count = legendre.shape[1]
    waves, tiles = lax.axis_size("wave"), lax.axis_size("tile")
    take = max(b for b in range(1, 17) if slots % b == 0)
    groups = slots // take
    smem = pl.BlockSpec(memory_space=pltpu.SMEM)
    vmem = pl.BlockSpec(memory_space=pltpu.VMEM)
    hbm = pl.BlockSpec(memory_space=pl.ANY)
    dma = pltpu.SemaphoreType.DMA((groups,))
    params = pltpu.CompilerParams(vmem_limit_bytes=60 * 2**20)
    coef = pl.pallas_call(
        functools.partial(forward_kernel, take),
        out_shape=jax.ShapeDtypeStruct((slots, 2 * lat_count, 2 * cols), BF16),
        in_specs=[smem, hbm, hbm],
        out_specs=vmem,
        scratch_shapes=[
            pltpu.VMEM(spectral.shape, BF16), pltpu.VMEM(legendre.shape, BF16), dma, dma,
        ],
        compiler_params=params,
        name="forward",
    )(pair_ids, spectral, legendre)
    coef = coef.reshape(slots, 2, waves, 2, 2, cols).transpose(2, 1, 4, 3, 5, 0)
    coef = coef.reshape(waves, 8 * cols, slots)
    back = middle(coef, pair_ids, waves, tiles, cols, lat_count)
    back = back.reshape(waves, 2, 2, 2, cols, slots).transpose(5, 2, 4, 1, 0, 3)
    back = back.reshape(slots, 2 * cols, 2 * lat_count)
    return pl.pallas_call(
        functools.partial(inverse_kernel, take),
        out_shape=jax.ShapeDtypeStruct(spectral.shape, BF16),
        in_specs=[smem, vmem, hbm],
        out_specs=hbm,
        scratch_shapes=[
            pltpu.VMEM(legendre.shape, BF16), pltpu.VMEM(spectral.shape, BF16), dma, dma,
        ],
        compiler_params=params,
        name="inverse",
    )(pair_ids, back, legendre)


def solution(mesh):
    placed = (P("wave", None, "tile", None), P("wave", None, None), P())
    return jax.shard_map(
        local, mesh=mesh, in_specs=placed, out_specs=P("wave", None, "tile", None), check_vma=False
    )
```

```python
import functools
import math

import jax
import jax.numpy as jnp
from jax import lax
from jax.experimental import pallas as pl
from jax.experimental.pallas import tpu as pltpu
from jax.sharding import PartitionSpec as P

MW = 1280
HALF_LATS = 1280
PAIRS = 640
NPTS = 5156
LANES = 128
RADIX = 32

F32 = jnp.float32
BF16 = jnp.bfloat16

HALF = MW // 2
GROUP = HALF // 2
GPAD = -(-GROUP // LANES) * LANES
BLOCKS = GPAD // RADIX
SPAN = 16
AHEAD = 3
MESH = pl.DeviceIdType.MESH
NT = (((1,), (1,)), ((), ()))


def dot(a, b):
    return jnp.dot(a, b, preferred_element_type=F32)


def dot_nt(a, b):
    return lax.dot_general(a, b, NT, preferred_element_type=F32)


def middle_kernel(waves, tiles, cols, lat_count, kpad, *refs):
    (coef, ids, out, fx, gsend, grecv, psend, precv, bsend, trig_t, small_c, small_s, hot,
     s1, r1, s2, r2, s3, r3, s4, r4) = refs
    wave, tile = lax.axis_index("wave"), lax.axis_index("tile")
    quarter = NPTS // 4
    halves = 4 * kpad // tiles
    per_d = tiles // 4
    rows = 2 * cols
    slots = coef.shape[2]

    def exchange(axis, here, count, src, dst, send, recv):
        copies = []
        for off in range(1, count):
            peer = lax.rem(here + off, count)
            copy = pltpu.make_async_remote_copy(
                src_ref=src.at[peer], dst_ref=dst.at[here], send_sem=send.at[off],
                recv_sem=recv.at[off], device_id={axis: peer}, device_id_type=MESH,
            )
            copy.start()
            copies.append(copy)
        dst[here] = src[here]
        return copies

    def finish(axis, here, count, src, dst, send, recv):
        for off in range(1, count):
            origin = lax.rem(here + count - off, count)
            pltpu.make_async_remote_copy(
                src_ref=src.at[origin], dst_ref=dst.at[origin], send_sem=send.at[off],
                recv_sem=recv.at[off], device_id={axis: origin}, device_id_type=MESH,
            ).wait_recv()

    barrier = pltpu.get_barrier_semaphore()
    for axis, here, count in (("wave", wave, waves), ("tile", tile, tiles)):
        for off in range(1, count):
            pl.semaphore_signal(
                barrier, inc=1, device_id={axis: lax.rem(here + off, count)}, device_id_type=MESH
            )

    polar = wave * HALF // (lat_count // 2)
    q0 = 5 + polar
    n0, n1 = 4 * q0, NPTS - 4 * q0

    def line(shape, axis):
        return lax.broadcasted_iota(jnp.int32, shape, axis)

    k = line((1, kpad), 1)
    second = k >= q0
    inside = k < quarter
    point = jnp.where(inside, k - jnp.where(second, q0, 0), 0).astype(F32)
    length = jnp.where(second, n1, n0).astype(F32)

    def trig(m):
        whole = m.astype(F32) * point
        phase = whole - jnp.floor(whole / length) * length
        angle = (2.0 * math.pi) * phase / length
        return jnp.cos(angle), jnp.sin(angle)

    r = line((RADIX, 1), 0)
    m = jnp.where(r < 8, 2 * r, 16 * (r - 8))
    m = jnp.where(r >= 12, (r - 12) // 2 * HALF + (r - 12) % 2, m)
    m = jnp.where(r >= 16, 2 * RADIX * (r - 16), m)
    c, s = trig(m)
    outer = 4 * SPAN
    for g in range(4):
        ca, sa, cb, sb = c[16:], s[16:], c[12 + g : 13 + g], s[12 + g : 13 + g]
        small_c[g * SPAN : (g + 1) * SPAN] = ca * cb - sa * sb
        small_s[g * SPAN : (g + 1) * SPAN] = sa * cb + ca * sb
        ca, sa, cb, sb = c[:8], s[:8], c[8 + g : 9 + g], s[8 + g : 9 + g]
        small_c[outer + 8 * g : outer + 8 * g + 8] = ca * cb - sa * sb
        small_s[outer + 8 * g : outer + 8 * g + 8] = sa * cb + ca * sb

    pl.semaphore_wait(barrier, waves + tiles - 2)
    sends = exchange("wave", wave, waves, coef, fx, s1, r1)

    def block(idx, carry):
        g, a = idx // BLOCKS, idx % BLOCKS
        row_a = g * SPAN + a
        ac, as_ = small_c[pl.ds(row_a, 1), :], small_s[pl.ds(row_a, 1), :]
        bc, bs = small_c[outer:, :], small_s[outer:, :]
        at = ((g % 2) * 4 + g // 2) * GPAD + a * RADIX
        cos_at = pl.ds(pl.multiple_of(at, RADIX), RADIX)
        sin_at = pl.ds(pl.multiple_of(at + 2 * GPAD, RADIX), RADIX)
        trig_t[cos_at, :] = (ac * bc - as_ * bs).astype(BF16)
        trig_t[sin_at, :] = (as_ * bc + ac * bs).astype(BF16)
        return carry

    lax.fori_loop(0, 4 * BLOCKS, block, 0)

    lane = line((2 * GPAD, 1), 0)
    par = jnp.where(lane >= GPAD, 1, 0)
    i = lane - par * GPAD
    low = jnp.where(i < GROUP, 2 * i + par, -1)
    high = jnp.where(i < GROUP, HALF - 1 - par - 2 * i, -1)
    pair = ids[...].reshape(1, ids.shape[0])
    hot[0] = jnp.where(pair == low, 1.0, 0.0).astype(BF16)
    hot[1] = jnp.where(pair == high, 1.0, 0.0).astype(BF16)

    row = line((rows, 1), 0)
    n_row = jnp.where(row >= cols, n1, n0)
    cycle = jnp.where(row >= cols, HALF_LATS - 1 - polar, polar)
    weight = 40.0 * jnp.sin(math.pi * (cycle.astype(F32) + 0.5) / (2.0 * HALF_LATS))
    weight = weight / jnp.sqrt(lat_count * n_row.astype(F32))
    ii = line((1, GPAD), 1)
    up = ii % 2 == 0
    sign = jnp.where(up, 1.0, -1.0)

    def wavenumber(h, p):
        return h * HALF + p + 2 * ii

    def table(p):
        return trig_t[p * 4 * GPAD : (p + 1) * 4 * GPAD, :]

    finish("wave", wave, waves, coef, fx, s1, r1)
    terms = [[[], []], [[], []]]
    for h in range(2):
        here = [fx[w, h * 2 * rows : (h + 1) * 2 * rows, :] for w in range(waves)]
        both = dot_nt(jnp.concatenate(here, axis=1), hot[h])
        for p in range(2):
            m = wavenumber(h, p)
            factor = jnp.where(2 * m < n_row, jnp.where(m == 0, 1.0, 2.0), 0.0)
            part = both[:, p * GPAD : (p + 1) * GPAD]
            re, im = part[:rows] * factor, part[rows:] * factor
            cos_side, sin_side = ((re, re), (-im, -im)) if p == 0 else ((re, im), (-im, re))
            for x, (a, b) in enumerate((cos_side, sin_side)):
                terms[p][x].append(jnp.concatenate([a, b * sign]).astype(BF16))
    even = dot(jnp.concatenate(terms[0][0] + terms[0][1], axis=1), table(0))
    odd = dot(jnp.concatenate(terms[1][0] + terms[1][1], axis=1), table(1))

    def lat_of(x, v):
        return jnp.where(
            second, x[v * rows + cols : (v + 1) * rows], x[v * rows : v * rows + cols]
        )

    e0, e1, o0, o1 = lat_of(even, 0), lat_of(even, 1), lat_of(odd, 0), lat_of(odd, 1)
    for d, x in enumerate((e0 + o0, e1 - o1, e0 - o0, e1 + o1)):
        x = x.astype(BF16)
        for t in range(per_d):
            gsend[d * per_d + t] = x[:, t * halves : (t + 1) * halves]
    sends += exchange("tile", tile, tiles, gsend, grecv, s2, r2)
    finish("tile", tile, tiles, gsend, grecv, s2, r2)

    layers = cols * tiles // 4
    per_f = tiles // 4

    def field(f):
        return jnp.concatenate([grecv[f * per_f + t] for t in range(per_f)])

    u, w_, q = field(0).astype(F32), field(1).astype(F32), field(3).astype(F32)
    t16 = field(2)
    tri = jnp.where(line((layers, layers), 1) >= line((layers, layers), 0), 1.0, 0.0)
    geo = dot(tri.astype(BF16), t16) / math.sqrt(layers)
    temp = t16.astype(F32)
    for f, x in enumerate((0.5 * (u * u + w_ * w_) + geo, u * temp, w_ * temp, u * q)):
        x = x.astype(BF16)
        for t in range(per_f):
            psend[f * per_f + t] = x[t * cols : (t + 1) * cols]
    sends += exchange("tile", tile, tiles, psend, precv, s3, r3)
    finish("tile", tile, tiles, psend, precv, s3, r3)

    def quadrant(d):
        x = jnp.concatenate([precv[d * per_d + t].astype(F32) for t in range(per_d)], axis=1)
        return jnp.where(inside, x, 0.0)

    x0, x1, x2, x3 = [quadrant(d) for d in range(4)]

    def by_lat(*variants):
        return jnp.concatenate(
            [jnp.where(keep, v, 0.0) for v in variants for keep in (k < q0, second)]
        ).astype(BF16)

    even_in = by_lat((x0 + x2) + (x1 + x3), (x0 + x2) - (x1 + x3))
    odd_in = by_lat(x0 - x2, x1 - x3)
    even_out, odd_out = dot_nt(even_in, table(0)), dot_nt(odd_in, table(1))
    for h in range(2):
        at_c, at_s = slice(h * GPAD, (h + 1) * GPAD), slice((2 + h) * GPAD, (3 + h) * GPAD)
        ec, es, oc, os_ = even_out[:, at_c], even_out[:, at_s], odd_out[:, at_c], odd_out[:, at_s]
        keep_e = jnp.where(2 * wavenumber(h, 0) < n_row, weight, 0.0)
        keep_o = jnp.where(2 * wavenumber(h, 1) < n_row, weight, 0.0)
        e_re = jnp.where(up, ec[:rows], ec[rows:]) * keep_e
        e_im = -jnp.where(up, es[:rows], es[rows:]) * keep_e
        o_re = (oc[:rows] - sign * os_[rows:]) * keep_o
        o_im = (-os_[:rows] - sign * oc[rows:]) * keep_o
        e_both = jnp.concatenate([e_re, e_im]).astype(BF16)
        o_both = jnp.concatenate([o_re, o_im]).astype(BF16)
        res = (dot(e_both, hot[h, :GPAD]) + dot(o_both, hot[h, GPAD:])).astype(BF16)
        for w in range(waves):
            bsend[w, h * 2 * rows : (h + 1) * 2 * rows, :] = res[:, w * slots : (w + 1) * slots]
    sends += exchange("wave", wave, waves, bsend, out, s4, r4)
    finish("wave", wave, waves, bsend, out, s4, r4)
    for copy in sends:
        copy.wait_send()


def middle(coef, ids, waves, tiles, cols, lat_count):
    slots = coef.shape[2]
    step = max(tiles // 4, 1) * LANES
    kpad = -(-(NPTS // 4) // step) * step
    chunk = (tiles, cols, 4 * kpad // tiles)
    dma = pltpu.SemaphoreType.DMA
    vmem = pl.BlockSpec(memory_space=pltpu.VMEM)
    return pl.pallas_call(
        functools.partial(middle_kernel, waves, tiles, cols, lat_count, kpad),
        out_shape=jax.ShapeDtypeStruct(coef.shape, BF16),
        in_specs=[vmem, vmem],
        out_specs=vmem,
        scratch_shapes=[
            pltpu.VMEM(coef.shape, BF16),
            pltpu.VMEM(chunk, BF16), pltpu.VMEM(chunk, BF16),
            pltpu.VMEM(chunk, BF16), pltpu.VMEM(chunk, BF16),
            pltpu.VMEM(coef.shape, BF16),
            pltpu.VMEM((8 * GPAD, kpad), BF16),
            pltpu.VMEM((4 * SPAN + RADIX, kpad), F32),
            pltpu.VMEM((4 * SPAN + RADIX, kpad), F32),
            pltpu.VMEM((2, 2 * GPAD, waves * slots), BF16),
            dma((waves,)), dma((waves,)), dma((tiles,)), dma((tiles,)),
            dma((tiles,)), dma((tiles,)), dma((waves,)), dma((waves,)),
        ],
        compiler_params=pltpu.CompilerParams(
            collective_id=0, has_side_effects=True, vmem_limit_bytes=40 * 2**20
        ),
        name="middle",
    )(coef, ids)


def halves_of(ids, block, base):
    lane = lax.broadcasted_iota(jnp.int32, block.shape[1:], 1)
    parts = []
    for b in range(block.shape[0]):
        rows = block[b].astype(F32)
        low = lane < MW - ids[base + b]
        both = [jnp.where(low, rows, 0.0), jnp.where(low, 0.0, rows)]
        parts.append(jnp.concatenate(both).astype(BF16))
    return jnp.concatenate(parts)


def same_slot(shape, rows, columns):
    row = lax.broadcasted_iota(jnp.int32, shape, 0) // rows
    return row == lax.broadcasted_iota(jnp.int32, shape, 1) // columns


def fold(rows, columns):
    row = lax.broadcasted_iota(jnp.int32, (rows, columns), 0) % columns
    same = row == lax.broadcasted_iota(jnp.int32, (rows, columns), 1)
    return jnp.where(same, 1.0, 0.0).astype(BF16)


def forward_kernel(take, ids, spectral, legendre, out, spec_v, leg_v, spec_sem, leg_sem):
    slots, lats, row_total = legendre.shape
    fields = spectral.shape[1] * spectral.shape[2]
    base = lax.axis_index("wave") * slots
    copies = []
    for g in range(slots // take):
        at = pl.ds(g * take, take)
        pair = [
            pltpu.make_async_copy(legendre.at[at], leg_v.at[at], leg_sem.at[g]),
            pltpu.make_async_copy(spectral.at[at], spec_v.at[at], spec_sem.at[g]),
        ]
        copies.append(pair)
    for pair in copies[:AHEAD]:
        for copy in pair:
            copy.start()
    shape = (take * 2 * lats, take * fields)
    same = same_slot(shape, 2 * lats, fields)
    folded = fold(take * fields, fields)
    for g, pair in enumerate(copies):
        for copy in pair:
            copy.wait()
        for copy in copies[g + AHEAD] if g + AHEAD < len(copies) else ():
            copy.start()
        here = slice(g * take, (g + 1) * take)
        left = halves_of(ids, leg_v[here], base + g * take)
        right = spec_v[here].astype(F32).reshape(take * fields, row_total).astype(BF16)
        full = jnp.where(same, dot_nt(left, right), 0.0).astype(BF16)
        full = dot(full, folded).astype(BF16)
        out[here] = full.reshape((take,) + out.shape[1:])


def inverse_kernel(take, ids, back, legendre, out, leg_v, out_v, leg_sem, out_sem):
    slots, lats, row_total = legendre.shape
    fields = out.shape[1] * out.shape[2]
    base = lax.axis_index("wave") * slots
    copies = []
    for g in range(slots // take):
        at = pl.ds(g * take, take)
        copies.append(pltpu.make_async_copy(legendre.at[at], leg_v.at[at], leg_sem.at[g]))
        copies[-1].start()
    shape = (take * fields, take * 2 * lats)
    same = same_slot(shape, fields, 2 * lats)
    folded = fold(take * 2 * lats, 2 * lats)
    results = []
    for g, copy in enumerate(copies):
        at = pl.ds(g * take, take)
        here = slice(g * take, (g + 1) * take)
        narrow = back[here].reshape(take * fields, 2 * lats)
        wide = jnp.where(same, dot_nt(narrow, folded), 0.0).astype(BF16)
        copy.wait()
        right = halves_of(ids, leg_v[here], base + g * take)
        out_v[here] = dot(wide, right).reshape((take,) + out.shape[1:]).astype(BF16)
        results.append(pltpu.make_async_copy(out_v.at[at], out.at[at], out_sem.at[g]))
        results[-1].start()
    for copy in results:
        copy.wait()


def local(spectral, legendre, pair_ids):
    slots, _, cols, row_total = spectral.shape
    lat_count = legendre.shape[1]
    waves, tiles = lax.axis_size("wave"), lax.axis_size("tile")
    take = max(b for b in range(1, 17) if slots % b == 0)
    groups = slots // take
    smem = pl.BlockSpec(memory_space=pltpu.SMEM)
    vmem = pl.BlockSpec(memory_space=pltpu.VMEM)
    hbm = pl.BlockSpec(memory_space=pl.ANY)
    dma = pltpu.SemaphoreType.DMA((groups,))
    params = pltpu.CompilerParams(vmem_limit_bytes=60 * 2**20)
    coef = pl.pallas_call(
        functools.partial(forward_kernel, take),
        out_shape=jax.ShapeDtypeStruct((slots, 2 * lat_count, 2 * cols), BF16),
        in_specs=[smem, hbm, hbm],
        out_specs=vmem,
        scratch_shapes=[
            pltpu.VMEM(spectral.shape, BF16), pltpu.VMEM(legendre.shape, BF16), dma, dma,
        ],
        compiler_params=params,
        name="forward",
    )(pair_ids, spectral, legendre)
    coef = coef.reshape(slots, 2, waves, 2, 2, cols).transpose(2, 1, 4, 3, 5, 0)
    coef = coef.reshape(waves, 8 * cols, slots)
    back = middle(coef, pair_ids, waves, tiles, cols, lat_count)
    back = back.reshape(waves, 2, 2, 2, cols, slots).transpose(5, 2, 4, 1, 0, 3)
    back = back.reshape(slots, 2 * cols, 2 * lat_count)
    return pl.pallas_call(
        functools.partial(inverse_kernel, take),
        out_shape=jax.ShapeDtypeStruct(spectral.shape, BF16),
        in_specs=[smem, vmem, hbm],
        out_specs=hbm,
        scratch_shapes=[
            pltpu.VMEM(legendre.shape, BF16), pltpu.VMEM(spectral.shape, BF16), dma, dma,
        ],
        compiler_params=params,
        name="inverse",
    )(pair_ids, back, legendre)


def solution(mesh):
    placed = (P("wave", None, "tile", None), P("wave", None, None), P())
    return jax.shard_map(
        local, mesh=mesh, in_specs=placed, out_specs=P("wave", None, "tile", None), check_vma=False
    )
```
